256 devices in a mesh: snap: 64 (over x, y, z_hi), feat: 4 (over z_lo, core).
Axes of the slice: x: 4, y: 4, z: 8 (z_hi: 4, z_lo: 2; z = z_hi * 2 + z_lo), core: 2. Of those that a mesh axis runs over, the one named last changes fastest.
Arguments:
- features: bfloat16 [64, 2048, 1024], P('snap', None, 'feat'), may hold values from -6 to 6
- block_index: int32 [64, 16, 8], P('snap'), may hold values from 0 to 15
- block_values: bfloat16 [64, 16, 8, 128, 128], P('snap'), may hold values from -0.1875 to 0.1875
- hop_in: bfloat16 [1024, 1024], P(None, 'feat'), may hold values from -0.1875 to 0.1875
- query_w: bfloat16 [1024, 1024], P(None, 'feat'), may hold values from -0.1875 to 0.1875
- key_w: bfloat16 [1024, 1024], P(None, 'feat'), may hold values from -0.1875 to 0.1875
- value_w: bfloat16 [1024, 1024], P(None, 'feat'), may hold values from -0.1875 to 0.1875
- output_w: bfloat16 [1024, 1024], P(None, 'feat'), may hold values from -0.1875 to 0.1875
- hop_out: bfloat16 [1024, 1024], P(None, 'feat'), may hold values from -0.1875 to 0.1875
- time_bias: float32 [64, 64], replicated, may hold values from -2 to 403
Outputs:
- result: bfloat16 [64, 2048, 1024], P('snap', None, 'feat')
The draws below stay inside these ranges and needn't reach their ends.
All inputs are finite; a program needn't handle non-finite values.
Results may differ from the reference program's by a relative error of at most 0.012.
Values may be sent and summed in bfloat16 or wider, within the bound.
No kernel may reach another device: no remote copies, remote signals or barrier semaphores. Data moves between devices by JAX's collectives and lax.ppermute only.
A program may use at most 64 MiB of HBM per device.

```python
import math
import jax
import jax.numpy as jnp
from jax import lax

VERT = 2048
FEAT = 1024
BLK = 128
NBR = 8
SNAPS = 64


def draw_time_bias(key, part):
    key_base = jax.random.fold_in(key, 0)
    base = jax.random.uniform(key_base, (SNAPS, SNAPS), jnp.float32, -2.0, 2.0)
    return base


def plant(entries, rng, least, high):
    extent = entries.shape
    spot = [jax.random.randint(jax.random.fold_in(rng, axis), (), 0, extent[axis]) for axis in range(len(extent))]
    entries = entries.at[tuple(spot)].set(least)
    longest = extent.index(max(extent))
    spot[longest] = (spot[longest] + 1) % extent[longest]
    return entries.at[tuple(spot)].set(high)


def steps_of(key, dims, cuts, smallest, top_value):
    factor_of, own = 1.0, jax.random.fold_in(key, 6)
    for position, blocks in cuts:
        heights = jnp.exp(jax.random.uniform(jax.random.fold_in(own, position), (blocks,), jnp.float32, smallest / len(cuts), top_value / len(cuts)))
        factor_of = factor_of * jnp.repeat(heights, dims[position] // blocks).reshape([-1 if axis == position else 1 for axis in range(len(dims))])
    return factor_of


def gaussian(key, extent, width, limit, cuts=(), dtype=jnp.bfloat16):
    gain = steps_of(key, extent, cuts, -0.22, 0.18) if cuts else 1.0
    drawn = jax.random.normal(key, extent, jnp.float32) * width * gain
    return jnp.minimum(jnp.maximum(drawn, -limit), limit).astype(dtype)


def setup_inputs(seed: int = 0) -> dict:
    splits = jax.random.split(jax.random.key(seed), 11)
    features = gaussian(splits[0], (SNAPS, VERT, FEAT), 1.0, 6.0, ((0, 64), (2, 4)))
    block_index = plant(jax.random.randint(splits[1], (SNAPS, VERT // BLK, NBR), 0, VERT // BLK), jax.random.fold_in(splits[1], 1), 0, (VERT // BLK) - 1).astype(jnp.int32)
    block_values = gaussian(splits[2], (SNAPS, VERT // BLK, NBR, BLK, BLK), (NBR * BLK) ** -0.5, 0.1875, ((0, 64),))
    hop_in = gaussian(splits[3], (FEAT, FEAT), FEAT ** -0.5, 0.1875, ((1, 4),))
    query_w = gaussian(splits[4], (FEAT, FEAT), FEAT ** -0.5, 0.1875, ((1, 4),))
    key_w = gaussian(splits[5], (FEAT, FEAT), FEAT ** -0.5, 0.1875, ((1, 4),))
    value_w = gaussian(splits[6], (FEAT, FEAT), FEAT ** -0.5, 0.1875, ((1, 4),))
    output_w = gaussian(splits[7], (FEAT, FEAT), FEAT ** -0.5, 0.1875, ((1, 4),))
    hop_out = gaussian(splits[8], (FEAT, FEAT), FEAT ** -0.5, 0.1875, ((1, 4),))
    time_bias = draw_time_bias(jax.random.fold_in(splits[10], 71), 0)
    return {"features": features, "block_index": block_index, "block_values": block_values, "hop_in": hop_in, "query_w": query_w, "key_w": key_w, "value_w": value_w, "output_w": output_w, "hop_out": hop_out, "time_bias": time_bias}


def aggregate(field, block_index, block_values):

    def one_snapshot(packed):
        plane, index_row, value_row = packed
        blocks = plane.reshape(VERT // BLK, BLK, FEAT).astype(jnp.float32)
        picked = blocks[index_row]
        summed = jnp.einsum('rkij,rkjc->ric', value_row.astype(jnp.float32), picked)
        return summed.reshape(VERT, FEAT).astype(jnp.bfloat16)
    return lax.map(one_snapshot, (field, block_index, block_values))

def dense(field, weight):
    flat = field.reshape(-1, field.shape[-1])
    product = jnp.dot(flat, weight, preferred_element_type=jnp.float32)
    return product.reshape(field.shape[:-1] + (weight.shape[1],))

def reference(features, block_index, block_values, hop_in, query_w, key_w, value_w, output_w, hop_out, time_bias):
    score_scale = 1.0 / math.sqrt(FEAT)
    agg_first = aggregate(features, block_index, block_values)
    hidden = jax.nn.relu(dense(agg_first, hop_in)).astype(jnp.bfloat16)
    query = dense(hidden, query_w).astype(jnp.bfloat16)
    keys = dense(hidden, key_w).astype(jnp.bfloat16)
    values = dense(hidden, value_w).astype(jnp.bfloat16)
    scores = jnp.einsum('tuc,suc->uts', query.astype(jnp.float32), keys.astype(jnp.float32)) * score_scale + time_bias[None]
    shifted = scores - lax.optimization_barrier(jnp.max(scores, axis=2, keepdims=True))
    weights = jnp.exp(shifted)
    probs = (weights / lax.optimization_barrier(jnp.sum(weights, axis=2, keepdims=True))).astype(jnp.bfloat16)
    context = jnp.einsum('uts,suc->tuc', probs.astype(jnp.float32), values.astype(jnp.float32)).astype(jnp.bfloat16)
    mixed = (hidden.astype(jnp.float32) + dense(context, output_w)).astype(jnp.bfloat16)
    agg_second = aggregate(mixed, block_index, block_values)
    return jax.nn.relu(dense(agg_second, hop_out)).astype(jnp.bfloat16)
```

```python
import math

import jax
import jax.numpy as jnp
from jax import lax
from jax.experimental import pallas as pl
from jax.experimental.pallas import tpu as pltpu
from jax.sharding import Mesh
from jax.sharding import PartitionSpec as P

VERT, FEAT, BLK, NBR, SNAPS = 2048, 1024, 128, 8, 64
ROWS = VERT // BLK
GROUP = 4
COLS = FEAT // GROUP
DEVS = SNAPS * GROUP
OWN = VERT // DEVS
LOCAL = SNAPS * OWN
AXES = ("x", "y", "zh", "zl", "core")
ORDER = ("zl", "core", "x", "y", "zh")
F32, BF16 = jnp.float32, jnp.bfloat16
STEP = 8


def hop_body(relu, index, field, blocks, out):
    step = pl.program_id(0)
    for i in range(STEP):
        picked, left = [], []
        for k in range(NBR):
            start = pl.multiple_of(index[(step * STEP + i) * NBR + k] * BLK, BLK)
            picked.append(field[pl.ds(start, BLK), :])
            left.append(blocks[i, k])
        total = jnp.dot(
            jnp.concatenate(left, axis=1),
            jnp.concatenate(picked, axis=0),
            preferred_element_type=F32,
        )
        if relu:
            total = jnp.maximum(total, 0.0)
        out[i * BLK : (i + 1) * BLK, :] = total.astype(BF16)


def hop(field, index, blocks, relu):
    def body(*refs):
        hop_body(relu, *refs)

    return pl.pallas_call(
        body,
        out_shape=jax.ShapeDtypeStruct((VERT, COLS), BF16),
        grid_spec=pltpu.PrefetchScalarGridSpec(
            num_scalar_prefetch=1,
            grid=(ROWS // STEP,),
            in_specs=[
                pl.BlockSpec((VERT, COLS), lambda r, ix: (0, 0)),
                pl.BlockSpec((STEP, NBR, BLK, BLK), lambda r, ix: (r, 0, 0, 0)),
            ],
            out_specs=pl.BlockSpec((STEP * BLK, COLS), lambda r, ix: (r, 0)),
        ),
        name="hop_relu" if relu else "hop",
    )(index, field, blocks)


def middle_body(scale, own, bias, got, *refs):
    pieces, out = refs[:24], refs[24]
    w, hidden, query, keys, values, table, sems = refs[25:]
    me = own[0]
    copies = []
    for i in range(6):
        row = []
        for g in range(4):
            place = jnp.bitwise_xor(me, g)
            row.append(pltpu.make_async_copy(pieces[i * 4 + g], w.at[i, place], sems.at[i, g]))
        copies.append(row)
    for row in copies:
        for copy in row:
            copy.start()

    def block(g):
        return slice(g * COLS, (g + 1) * COLS)

    def dot(a, b):
        return jnp.dot(a, b, preferred_element_type=F32)

    def arrive(i):
        for copy in copies[i]:
            copy.wait()

    rest, spread = bias[...], None
    at = lax.broadcasted_iota(jnp.int32, (LOCAL, SNAPS), 0) // OWN
    onehot = (at == lax.broadcasted_iota(jnp.int32, (LOCAL, SNAPS), 1)).astype(F32).astype(BF16)
    for _ in range(3):
        part = rest.astype(BF16)
        rest = rest - part.astype(F32)
        rows = dot(onehot, part).astype(BF16)
        part = lax.dot_general(rows, onehot, (((1,), (1,)), ((), ())), preferred_element_type=F32)
        spread = part if spread is None else spread + part
    vertex = lax.broadcasted_iota(jnp.int32, (LOCAL, LOCAL), 0) % OWN
    other = lax.broadcasted_iota(jnp.int32, (LOCAL, LOCAL), 1) % OWN
    table[...] = jnp.where(vertex == other, spread, -jnp.inf)

    agg = jnp.concatenate([got[g] for g in range(4)], axis=1)
    arrive(0)
    for g in range(4):
        hidden[:, block(g)] = jnp.maximum(dot(agg, w[0, g]), 0.0).astype(BF16)
    for i, ref in ((1, query), (2, keys), (3, values)):
        arrive(i)
        for g in range(4):
            ref[:, block(g)] = dot(hidden[...], w[i, g]).astype(BF16)
    logits = (
        lax.dot_general(query[...], keys[...], (((1,), (1,)), ((), ())), preferred_element_type=F32)
        * scale
        + table[...]
    )
    weights = jnp.exp(logits - jnp.max(logits, axis=1, keepdims=True))
    probs = (weights / jnp.sum(weights, axis=1, keepdims=True)).astype(BF16)
    for g in range(4):
        query[:, block(g)] = dot(probs, values[:, block(g)]).astype(BF16)
    arrive(4)
    for g in range(4):
        update = dot(query[...], w[4, g])
        keys[:, block(g)] = (hidden[:, block(g)].astype(F32) + update).astype(BF16)
    arrive(5)
    for g in range(4):
        out[g] = dot(keys[...], w[5, g]).astype(BF16)


def middle(own, bias, got, pieces, scale):
    def body(*refs):
        middle_body(scale, *refs)

    vmem = pl.BlockSpec(memory_space=pltpu.VMEM)
    return pl.pallas_call(
        body,
        out_shape=jax.ShapeDtypeStruct((GROUP, LOCAL, COLS), BF16),
        in_specs=[pl.BlockSpec(memory_space=pltpu.SMEM), vmem, vmem]
        + [pl.BlockSpec(memory_space=pl.ANY)] * 24,
        out_specs=vmem,
        scratch_shapes=[pltpu.VMEM((6, GROUP, FEAT, COLS), BF16)]
        + [pltpu.VMEM((LOCAL, FEAT), BF16)] * 4
        + [pltpu.VMEM((LOCAL, LOCAL), F32), pltpu.SemaphoreType.DMA((6, GROUP))],
        name="middle",
    )(own, bias, got, *pieces)


def z_partner(up):
    pairs = []
    for zh in range(4):
        for zl in range(2):
            z = zh * 2 + zl
            there = (z + (1 if up else -1)) % 8
            pairs.append((z, there))
    return pairs


def local(features, block_index, block_values, hop_in, query_w, key_w, value_w, output_w, hop_out, time_bias):
    scale = 1.0 / math.sqrt(FEAT)
    weights = (hop_in, query_w, key_w, value_w, output_w, hop_out)
    swap = [(0, 1), (1, 0)]
    across = [lax.ppermute(w, ("zh", "zl"), z_partner(i % 2 == 0)) for i, w in enumerate(weights)]
    pieces = []
    for w, far in zip(weights, across):
        pieces += [w, lax.ppermute(w, "core", swap), far, lax.ppermute(far, "core", swap)]
    index = block_index.reshape(ROWS * NBR)
    blocks = block_values[0]
    own = (lax.axis_index("zl") * 2 + lax.axis_index("core")).astype(jnp.int32).reshape(1)

    agg = hop(features[0], index, blocks, False)
    got = lax.all_to_all(agg.reshape(DEVS, OWN, COLS), ORDER, 0, 0, tiled=True)
    sent = middle(own, time_bias, got.reshape(GROUP, LOCAL, COLS), pieces, scale)
    back = lax.all_to_all(sent.reshape(DEVS, OWN, COLS), ORDER, 0, 0, tiled=True)
    return hop(back.reshape(VERT, COLS), index, blocks, True)[None]


def solution(mesh):
    fine = Mesh(mesh.devices.reshape(4, 4, 4, 2, 2), AXES)
    snap, feat = ("x", "y", "zh"), ("zl", "core")
    in_specs = (
        P(snap, None, feat),
        P(snap, None, None),
        P(snap, None, None, None, None),
    ) + (P(None, feat),) * 6 + (P(),)
    return jax.shard_map(
        local, mesh=fine, in_specs=in_specs, out_specs=P(snap, None, feat), check_vma=False
    )
```

```python
import math

import jax
import jax.numpy as jnp
from jax import lax
from jax.experimental import pallas as pl
from jax.experimental.pallas import tpu as pltpu
from jax.sharding import Mesh
from jax.sharding import PartitionSpec as P


VERT, FEAT, BLK, NBR, SNAPS = 2048, 1024, 128, 8, 64
ROWS = VERT // BLK
GROUP = 4
COLS = FEAT // GROUP
DEVS = SNAPS * GROUP
HALF = FEAT // 2
QUART = FEAT // 4
OWN = VERT // DEVS
LOCAL = SNAPS * OWN
AXES = ("x", "y", "zh", "zl", "core")
ORDER = ("zl", "core", "x", "y", "zh")
F32, BF16 = jnp.float32, jnp.bfloat16
STEP = 8


def hop_body(relu, index, field, blocks, out):
    step = pl.program_id(0)
    for i in range(STEP):
        picked, left = [], []
        for k in range(NBR):
            start = pl.multiple_of(index[k, step * STEP + i] * BLK, BLK)
            picked.append(field[pl.ds(start, BLK), :])
            left.append(blocks[i, k])
        total = jnp.dot(
            jnp.concatenate(left, axis=1),
            jnp.concatenate(picked, axis=0),
            preferred_element_type=F32,
        )
        if relu:
            total = jnp.maximum(total, 0.0)
        out[i * BLK : (i + 1) * BLK, :] = total.astype(BF16)


def hop(field, index, blocks, relu):
    def body(*refs):
        hop_body(relu, *refs)

    return pl.pallas_call(
        body,
        out_shape=jax.ShapeDtypeStruct((VERT, COLS), BF16),
        grid_spec=pltpu.PrefetchScalarGridSpec(
            num_scalar_prefetch=1,
            grid=(ROWS // STEP,),
            in_specs=[
                pl.BlockSpec((VERT, COLS), lambda r, ix: (0, 0)),
                pl.BlockSpec((STEP, NBR, BLK, BLK), lambda r, ix: (r, 0, 0, 0)),
            ],
            out_specs=pl.BlockSpec((STEP * BLK, COLS), lambda r, ix: (r, 0)),
        ),
        name="hop_relu" if relu else "hop",
    )(index, field, blocks)


def middle_body(scale, own, bias, got, *refs):
    pieces, out = refs[:24], refs[24]
    w, hidden, query, keys, values, table, sems = refs[25:]
    me = own[0]
    copies = []
    for i in range(6):
        group, j = i // 3, i % 3
        half = own[1 + group]
        row = []

        def move(piece, block, start=None):
            place = w.at[i, jnp.bitwise_xor(me, block)]
            if start is not None:
                place = place.at[pl.ds(pl.multiple_of(start, QUART), QUART)]
            row.append(pltpu.make_async_copy(piece, place, sems.at[i, len(row)]))

        move(pieces[i], 0)
        move(pieces[6 + i], 1)
        for g in range(2):
            far, *sides = pieces[12 + group * 6 + g * 3 : 15 + group * 6 + g * 3]
            for sub in range(2):
                move(far.at[sub, j], 2 + g, half * HALF + sub * QUART)
                move(sides[sub].at[j], 2 + g, (1 - half) * HALF + sub * QUART)
        copies.append(row)
    for row in copies:
        for copy in row:
            copy.start()

    def block(g):
        return slice(g * COLS, (g + 1) * COLS)

    def dot(a, b):
        return jnp.dot(a, b, preferred_element_type=F32)

    def arrive(i):
        for copy in copies[i]:
            copy.wait()

    rest, spread = bias[...], None
    at = lax.broadcasted_iota(jnp.int32, (LOCAL, SNAPS), 0) // OWN
    onehot = (at == lax.broadcasted_iota(jnp.int32, (LOCAL, SNAPS), 1)).astype(F32).astype(BF16)
    for _ in range(3):
        part = rest.astype(BF16)
        rest = rest - part.astype(F32)
        rows = dot(onehot, part).astype(BF16)
        part = lax.dot_general(rows, onehot, (((1,), (1,)), ((), ())), preferred_element_type=F32)
        spread = part if spread is None else spread + part
    vertex = lax.broadcasted_iota(jnp.int32, (LOCAL, LOCAL), 0) % OWN
    other = lax.broadcasted_iota(jnp.int32, (LOCAL, LOCAL), 1) % OWN
    table[...] = jnp.where(vertex == other, spread, -jnp.inf)

    agg = jnp.concatenate([got[g] for g in range(4)], axis=1)
    arrive(0)
    for g in range(4):
        hidden[:, block(g)] = jnp.maximum(dot(agg, w[0, g]), 0.0).astype(BF16)
    for i, ref in ((1, query), (2, keys), (3, values)):
        arrive(i)
        for g in range(4):
            ref[:, block(g)] = dot(hidden[...], w[i, g]).astype(BF16)
    logits = (
        lax.dot_general(query[...], keys[...], (((1,), (1,)), ((), ())), preferred_element_type=F32)
        * scale
        + table[...]
    )
    weights = jnp.exp(logits - jnp.max(logits, axis=1, keepdims=True))
    probs = (weights / jnp.sum(weights, axis=1, keepdims=True)).astype(BF16)
    for g in range(4):
        query[:, block(g)] = dot(probs, values[:, block(g)]).astype(BF16)
    arrive(4)
    for g in range(4):
        update = dot(query[...], w[4, g])
        keys[:, block(g)] = (hidden[:, block(g)].astype(F32) + update).astype(BF16)
    arrive(5)
    for g in range(4):
        out[g] = dot(keys[...], w[5, g]).astype(BF16)


def middle(own, bias, got, pieces, scale):
    def body(*refs):
        middle_body(scale, *refs)

    vmem = pl.BlockSpec(memory_space=pltpu.VMEM)
    return pl.pallas_call(
        body,
        out_shape=jax.ShapeDtypeStruct((GROUP, LOCAL, COLS), BF16),
        in_specs=[pl.BlockSpec(memory_space=pltpu.SMEM), vmem, vmem]
        + [pl.BlockSpec(memory_space=pl.ANY)] * 24,
        out_specs=vmem,
        scratch_shapes=[pltpu.VMEM((6, GROUP, FEAT, COLS), BF16)]
        + [pltpu.VMEM((LOCAL, FEAT), BF16)] * 4
        + [pltpu.VMEM((LOCAL, LOCAL), F32), pltpu.SemaphoreType.DMA((6, 10))],
        name="middle",
    )(own, bias, got, *pieces)


def pack_body(half, *refs):
    inputs, outputs, sems = refs[:6], refs[6:8], refs[8]
    copies = []
    for i in range(6):
        start = half[i // 3] * HALF
        for sub in range(2):
            rows = pl.ds(pl.multiple_of(start + sub * QUART, QUART), QUART)
            place = outputs[i // 3].at[sub, i % 3]
            copies.append(pltpu.make_async_copy(inputs[i].at[rows], place, sems.at[i, sub]))
    for copy in copies:
        copy.start()
    for copy in copies:
        copy.wait()


def pack(half, weights):
    anywhere = pl.BlockSpec(memory_space=pl.ANY)
    return pl.pallas_call(
        pack_body,
        out_shape=[jax.ShapeDtypeStruct((2, 3, QUART, COLS), BF16)] * 2,
        in_specs=[pl.BlockSpec(memory_space=pltpu.SMEM)] + [anywhere] * 6,
        out_specs=[pl.BlockSpec(memory_space=pltpu.VMEM)] * 2,
        scratch_shapes=[pltpu.SemaphoreType.DMA((6, 2))],
        name="pack",
    )(half, *weights)


def z_partner(up):
    pairs = []
    for zh in range(4):
        for zl in range(2):
            z = zh * 2 + zl
            there = (z + (1 if up else -1)) % 8
            pairs.append((z, there))
    return pairs


def local(features, block_index, block_values, hop_in, query_w, key_w, value_w, output_w, hop_out, time_bias):
    scale = 1.0 / math.sqrt(FEAT)
    weights = (hop_in, query_w, key_w, value_w, output_w, hop_out)
    swap = [(0, 1), (1, 0)]
    halves = jnp.stack([lax.axis_index("x") % 2, lax.axis_index("y") % 2]).astype(jnp.int32)
    groups = pack(halves, weights)
    features, groups = lax.optimization_barrier((features, groups))
    far = []
    for g in range(2):
        far.append(lax.ppermute(groups[g], ("zh", "zl"), z_partner(g == 1)))
    swapped = [lax.ppermute(w, "core", swap) for w in weights]
    far, swapped = lax.optimization_barrier((far, swapped))
    pieces = list(weights) + list(swapped)
    even, odd = [(0, 1), (1, 0), (2, 3), (3, 2)], [(0, 3), (3, 0), (1, 2), (2, 1)]
    for g in range(2):
        sides = []
        for sub in range(2):
            sides.append(lax.ppermute(far[g][sub], "xy"[g], (even, odd)[sub]))
        far_swap = lax.ppermute(far[g], "core", swap)
        side_swap = [lax.ppermute(side, "core", swap) for side in sides]
        pieces += [far[g], *sides, far_swap, *side_swap]
    index = block_index[0].T
    blocks = block_values[0]
    place = lax.axis_index("zl") * 2 + lax.axis_index("core")
    own = jnp.concatenate([place.astype(jnp.int32).reshape(1), halves])

    agg = hop(features[0], index, blocks, False)
    got = lax.all_to_all(agg.reshape(DEVS, OWN, COLS), ORDER, 0, 0, tiled=True)
    sent = middle(own, time_bias, got.reshape(GROUP, LOCAL, COLS), pieces, scale)
    back = lax.all_to_all(sent.reshape(DEVS, OWN, COLS), ORDER, 0, 0, tiled=True)
    return hop(back.reshape(VERT, COLS), index, blocks, True)[None]


def solution(mesh):
    fine = Mesh(mesh.devices.reshape(4, 4, 4, 2, 2), AXES)
    snap, feat = ("x", "y", "zh"), ("zl", "core")
    in_specs = (
        P(snap, None, feat),
        P(snap, None, None),
        P(snap, None, None, None, None),
    ) + (P(None, feat),) * 6 + (P(),)

    return jax.shard_map(
        local, mesh=fine, in_specs=in_specs, out_specs=P(snap, None, feat), check_vma=False
    )
```

```python
import math

import jax
import jax.numpy as jnp
from jax import lax
from jax.experimental import pallas as pl
from jax.experimental.pallas import tpu as pltpu
from jax.sharding import Mesh
from jax.sharding import PartitionSpec as P


VERT, FEAT, BLK, NBR, SNAPS = 2048, 1024, 128, 8, 64
ROWS = VERT // BLK
GROUP = 4
COLS = FEAT // GROUP
DEVS = SNAPS * GROUP
HALF = FEAT // 2
QUART = FEAT // 4
OWN = VERT // DEVS
LOCAL = SNAPS * OWN
AXES = ("x", "y", "zh", "zl", "core")
ORDER = ("zl", "core", "x", "y", "zh")
F32, BF16 = jnp.float32, jnp.bfloat16
STEP = 8


def hop_body(relu, index, field, blocks, out):
    step = pl.program_id(0)
    for i in range(STEP):
        picked, left = [], []
        for k in range(NBR):
            start = pl.multiple_of(index[k, step * STEP + i] * BLK, BLK)
            picked.append(field[pl.ds(start, BLK), :])
            left.append(blocks[i, k])
        total = jnp.dot(
            jnp.concatenate(left, axis=1),
            jnp.concatenate(picked, axis=0),
            preferred_element_type=F32,
        )
        if relu:
            total = jnp.maximum(total, 0.0)
        out[i * BLK : (i + 1) * BLK, :] = total.astype(BF16)


def hop(field, index, blocks, relu):
    def body(*refs):
        hop_body(relu, *refs)

    return pl.pallas_call(
        body,
        out_shape=jax.ShapeDtypeStruct((VERT, COLS), BF16),
        grid_spec=pltpu.PrefetchScalarGridSpec(
            num_scalar_prefetch=1,
            grid=(ROWS // STEP,),
            in_specs=[
                pl.BlockSpec((VERT, COLS), lambda r, ix: (0, 0)),
                pl.BlockSpec((STEP, NBR, BLK, BLK), lambda r, ix: (r, 0, 0, 0)),
            ],
            out_specs=pl.BlockSpec((STEP * BLK, COLS), lambda r, ix: (r, 0)),
        ),
        name="hop_relu" if relu else "hop",
    )(index, field, blocks)


def middle_body(scale, bias, got, *refs):
    pieces, out = refs[:24], refs[24]
    w, hidden, query, keys, values, table, sems = refs[25:]
    me = lax.axis_index("zl") * 2 + lax.axis_index("core")
    halves = (lax.axis_index("x") % 2, lax.axis_index("y") % 2)
    copies = []
    for i in range(6):
        group, j = i // 3, i % 3
        half = halves[group]
        row = []

        def move(piece, block, start=None):
            place = w.at[i, jnp.bitwise_xor(me, block)]
            if start is not None:
                place = place.at[pl.ds(pl.multiple_of(start, QUART), QUART)]
            row.append(pltpu.make_async_copy(piece, place, sems.at[i, len(row)]))

        move(pieces[i], 0)
        move(pieces[6 + i], 1)
        for g in range(2):
            far, *sides = pieces[12 + group * 6 + g * 3 : 15 + group * 6 + g * 3]
            for sub in range(2):
                move(far.at[sub, j], 2 + g, half * HALF + sub * QUART)
                move(sides[sub].at[j], 2 + g, (1 - half) * HALF + sub * QUART)
        copies.append(row)
    for row in copies:
        for copy in row:
            copy.start()

    def block(g):
        return slice(g * COLS, (g + 1) * COLS)

    def dot(a, b):
        return jnp.dot(a, b, preferred_element_type=F32)

    def arrive(i):
        for copy in copies[i]:
            copy.wait()

    rest, spread = bias[...], None
    at = lax.broadcasted_iota(jnp.int32, (LOCAL, SNAPS), 0) // OWN
    onehot = (at == lax.broadcasted_iota(jnp.int32, (LOCAL, SNAPS), 1)).astype(F32).astype(BF16)
    for _ in range(3):
        part = rest.astype(BF16)
        rest = rest - part.astype(F32)
        rows = dot(onehot, part).astype(BF16)
        part = lax.dot_general(rows, onehot, (((1,), (1,)), ((), ())), preferred_element_type=F32)
        spread = part if spread is None else spread + part
    vertex = lax.broadcasted_iota(jnp.int32, (LOCAL, LOCAL), 0) % OWN
    other = lax.broadcasted_iota(jnp.int32, (LOCAL, LOCAL), 1) % OWN
    table[...] = jnp.where(vertex == other, spread, -jnp.inf)

    agg = jnp.concatenate([got[g] for g in range(4)], axis=1)
    arrive(0)
    for g in range(4):
        hidden[:, block(g)] = jnp.maximum(dot(agg, w[0, g]), 0.0).astype(BF16)
    for i, ref in ((1, query), (2, keys), (3, values)):
        arrive(i)
        for g in range(4):
            ref[:, block(g)] = dot(hidden[...], w[i, g]).astype(BF16)
    logits = (
        lax.dot_general(query[...], keys[...], (((1,), (1,)), ((), ())), preferred_element_type=F32)
        * scale
        + table[...]
    )
    weights = jnp.exp(logits - jnp.max(logits, axis=1, keepdims=True))
    probs = (weights / jnp.sum(weights, axis=1, keepdims=True)).astype(BF16)
    for g in range(4):
        query[:, block(g)] = dot(probs, values[:, block(g)]).astype(BF16)
    arrive(4)
    for g in range(4):
        update = dot(query[...], w[4, g])
        keys[:, block(g)] = (hidden[:, block(g)].astype(F32) + update).astype(BF16)
    arrive(5)
    for g in range(4):
        out[g] = dot(keys[...], w[5, g]).astype(BF16)


def middle(bias, got, pieces, scale):
    def body(*refs):
        middle_body(scale, *refs)

    vmem = pl.BlockSpec(memory_space=pltpu.VMEM)
    return pl.pallas_call(
        body,
        out_shape=jax.ShapeDtypeStruct((GROUP, LOCAL, COLS), BF16),
        in_specs=[vmem, vmem]
        + [pl.BlockSpec(memory_space=pl.ANY)] * 24,
        out_specs=vmem,
        scratch_shapes=[pltpu.VMEM((6, GROUP, FEAT, COLS), BF16)]
        + [pltpu.VMEM((LOCAL, FEAT), BF16)] * 4
        + [pltpu.VMEM((LOCAL, LOCAL), F32), pltpu.SemaphoreType.DMA((6, 10))],
        name="middle",
    )(bias, got, *pieces)


def pack_body(*refs):
    half = (lax.axis_index("x") % 2, lax.axis_index("y") % 2)
    inputs, outputs, sems = refs[:6], refs[6:8], refs[8]
    copies = []
    for i in range(6):
        start = half[i // 3] * HALF
        for sub in range(2):
            rows = pl.ds(pl.multiple_of(start + sub * QUART, QUART), QUART)
            place = outputs[i // 3].at[sub, i % 3]
            copies.append(pltpu.make_async_copy(inputs[i].at[rows], place, sems.at[i, sub]))
    for copy in copies:
        copy.start()
    for copy in copies:
        copy.wait()


def pack(weights):
    anywhere = pl.BlockSpec(memory_space=pl.ANY)
    return pl.pallas_call(
        pack_body,
        out_shape=[jax.ShapeDtypeStruct((2, 3, QUART, COLS), BF16)] * 2,
        in_specs=[anywhere] * 6,
        out_specs=[pl.BlockSpec(memory_space=pltpu.VMEM)] * 2,
        scratch_shapes=[pltpu.SemaphoreType.DMA((6, 2))],
        name="pack",
    )(*weights)


def z_partner(up):
    pairs = []
    for zh in range(4):
        for zl in range(2):
            z = zh * 2 + zl
            there = (z + (1 if up else -1)) % 8
            pairs.append((z, there))
    return pairs


def local(features, block_index, block_values, hop_in, query_w, key_w, value_w, output_w, hop_out, time_bias):
    scale = 1.0 / math.sqrt(FEAT)
    weights = (hop_in, query_w, key_w, value_w, output_w, hop_out)
    swap = [(0, 1), (1, 0)]
    groups = pack(weights)
    features, groups = lax.optimization_barrier((features, groups))
    far = []
    for g in range(2):
        far.append(lax.ppermute(groups[g], ("zh", "zl"), z_partner(g == 1)))
    swapped = [lax.ppermute(w, "core", swap) for w in weights]
    pieces = list(weights) + list(swapped)
    even, odd = [(0, 1), (1, 0), (2, 3), (3, 2)], [(0, 3), (3, 0), (1, 2), (2, 1)]
    for g in range(2):
        sides = []
        for sub in range(2):
            sides.append(lax.ppermute(far[g][sub], "xy"[g], (even, odd)[sub]))
        far_swap = lax.ppermute(far[g], "core", swap)
        side_swap = [lax.ppermute(side, "core", swap) for side in sides]
        pieces += [far[g], *sides, far_swap, *side_swap]
    index = block_index[0].T
    blocks = block_values[0]
    agg = hop(features[0], index, blocks, False)
    got = lax.all_to_all(agg.reshape(DEVS, OWN, COLS), ORDER, 0, 0, tiled=True)
    sent = middle(time_bias, got.reshape(GROUP, LOCAL, COLS), pieces, scale)
    back = lax.all_to_all(sent.reshape(DEVS, OWN, COLS), ORDER, 0, 0, tiled=True)
    return hop(back.reshape(VERT, COLS), index, blocks, True)[None]


def solution(mesh):
    fine = Mesh(mesh.devices.reshape(4, 4, 4, 2, 2), AXES)
    snap, feat = ("x", "y", "zh"), ("zl", "core")
    in_specs = (
        P(snap, None, feat),
        P(snap, None, None),
        P(snap, None, None, None, None),
    ) + (P(None, feat),) * 6 + (P(),)

    return jax.shard_map(
        local, mesh=fine, in_specs=in_specs, out_specs=P(snap, None, feat), check_vma=False
    )
```
